32 devices in a mesh: groups: 2 (over x), section: 2 (over core), expert: 8 (over z, y).
Axes of the slice: x: 2, y: 2, z: 4, core: 2. Of those that a mesh axis runs over, the one named last changes fastest.
Arguments:
- token_rows: bfloat16 [2, 256, 3072], P('section', ('groups', 'expert')), parts along dimension 1, may hold values from -36 to 36
- norm_gain: float32 [2, 3072], P('section'), may hold values from 0.1 to 1.9
- router: float32 [2, 3072, 4], P('section'), may hold values from -0.109375 to 0.109375
- w_gate: bfloat16 [2, 8, 3072, 4096], P('section', 'expert'), may hold values from -0.109375 to 0.109375
- w_up: bfloat16 [2, 8, 3072, 4096], P('section', 'expert'), may hold values from -0.109375 to 0.109375
- w_down: bfloat16 [2, 8, 4096, 3072], P('section', 'expert'), may hold values from -0.0625 to 0.0625
- routes: int32 [2, 256, 2], P('section', 'groups'), parts along dimension 1, may hold values from 0 to 3, all different within a row; in each aligned block of 16 rows (0 to 15, 16 to 31, ..., all dimensions but the last counted through in order) at most 16 rows name the same one
Outputs:
- next_rows: bfloat16 [2, 256, 3072], P('section', ('groups', 'expert')), parts along dimension 1
The draws below stay inside these ranges and needn't reach their ends.
There are 2 independent parts, one for each index of `groups`. The reference program is written for one: setup_inputs(seed, part) draws one part's arguments, and reference() takes and returns one part's arrays. A program takes and returns all parts, laid end to end along the dimension named above; an argument that names none is the same for every part. Nothing has to cross between parts.
Inputs may be any that keep to these rules, and one draw needn't show every extreme that they name: `routes`: the two experts of a row differ, and every expert is named by some row.
All inputs are finite; a program needn't handle non-finite values.
Results may differ from the reference program's by a relative error of at most 0.0026.
Values may be sent and summed in bfloat16 or wider, within the bound.
A program may use at most 192 MiB of HBM per device.

```python
import math
import jax
import jax.numpy as jnp
import numpy as np
from jax import lax

D = 3072
FF = 8192
EXPERTS = 4
ROWS_DEV = 16
SECTIONS = 2
SLICES = 2
FF_DEV = 4096
TOKENS = 128


def draw_token_rows(key, part):
    key_base, key_row, key_col = jax.random.split(key, 3)
    shape_all = (SECTIONS, TOKENS, D)
    base_value = jnp.clip(jax.random.normal(key_base, shape_all, jnp.float32), -4.0, 4.0)
    log_low = math.log(0.3)
    log_high = math.log(3.0)
    row_scale = jnp.exp(jax.random.uniform(key_row, (SECTIONS, TOKENS, 1), jnp.float32, log_low, log_high))
    col_scale = jnp.exp(jax.random.uniform(key_col, (SECTIONS, 1, D), jnp.float32, log_low, log_high))
    return jnp.clip(base_value * row_scale * col_scale, -36.0, 36.0).astype(jnp.bfloat16)


def level_of(own_key, dims, cuts, smallest, high):
    level = 1.0
    for position, parts in cuts:
        heights = jax.random.uniform(jax.random.fold_in(jax.random.fold_in(own_key, 6), position), (parts,), jnp.float32, smallest / len(cuts), high / len(cuts))
        level = level * jnp.repeat(jnp.exp(heights), dims[position] // parts).reshape((-1,) + (1,) * (len(dims) - 1 - position))
    return level


def routed_block(key, own, number, rows, amount, top, reach, skew):
    order = jax.random.permutation(key, amount)
    heavy_load, usual = shares(amount, rows * top, reach, skew, True), shares(amount, rows * top, reach, skew, False)
    places = jnp.arange(amount)

    def named(sizes, offset_by):
        used = int((sizes > 0).sum())
        fixed = max(1, used // 4)
        shifted = fixed + (places - fixed + offset_by * (used - fixed)) % max(1, amount - fixed)
        return jnp.zeros((amount,), jnp.int32).at[order[jnp.where(places < fixed, places, shifted)]].set(jnp.asarray(sizes, jnp.int32))

    sizes = jnp.where(number % 4 == 0, named(heavy_load, number // 4), named(usual, number - number // 4 - 1))
    mixed = jax.random.permutation(jax.random.fold_in(own, 3), amount)
    source_of, receiver = mixed[0:amount // 2 * 2:2], mixed[1:amount // 2 * 2:2]
    room = jnp.minimum(sizes[source_of] - 1, reach - sizes[receiver]) // 2
    room = jnp.where((source_of == order[0]) | (receiver == order[0]) | (sizes[receiver] == 0), 0, jnp.maximum(room, 0))
    shifted = jax.random.randint(jax.random.fold_in(own, 4), (amount // 2,), 0, 1 << 20) % (room + 1)
    sizes = sizes.at[source_of].add(-shifted).at[receiver].add(shifted)
    labels = jnp.searchsorted(jnp.cumsum(sizes), jnp.arange(rows * top), side="right").astype(jnp.int32)
    table = labels.reshape(top, rows).T
    table = table[jax.random.permutation(jax.random.fold_in(own, 1), rows)]
    offset_by = jax.random.randint(jax.random.fold_in(own, 2), (rows, 1), 0, top)
    return jnp.take_along_axis(table, (jnp.arange(top)[None, :] + offset_by) % top, axis=1)


def shares(count, total, most, skew, full):
    loads = [(1 << 20) // math.isqrt(grade ** skew) + 1 for grade in range(1, count + 1)]
    largest = most if full else min(most, max(-(-total // count), total * loads[0] // sum(loads)))
    least = 1 if total - largest >= count - 1 else 0
    given, surplus = [largest] + [least] * (count - 1), total - largest - least * (count - 1)
    while surplus > 0:
        movable = [i for i in range(1, count) if given[i] < largest] or [i for i in range(1, count) if given[i] < most]
        whole, remaining = sum([loads[i] for i in movable]), surplus
        for i in movable:
            addition = min(most - given[i], max(1, remaining * loads[i] // whole), surplus)
            given[i] = given[i] + addition
            surplus = surplus - addition
    return np.array(given)


def bell_draw(stream_key, extent, deviation, limit, shards=(), kind=jnp.bfloat16):
    array = jax.random.normal(stream_key, extent, jnp.float32) * deviation
    if len(shards) > 0:
        array = level_of(stream_key, extent, shards, -0.22, 0.18) * array
    return jnp.clip(array, min=-limit, max=limit).astype(kind)


def setup_inputs(seed: int = 0, part: int = 0) -> dict:
    splits = jax.random.split(jax.random.key(seed), 8)
    own_keys = jax.random.split(jax.random.fold_in(splits[7], part), 8)
    token_rows = draw_token_rows(jax.random.fold_in(jax.random.fold_in(splits[7], part), 71), part)
    norm_gain = jnp.clip(1.0 + 0.18 * jax.random.normal(splits[1], (SECTIONS, D), jnp.float32), 0.1, 1.9)
    router = bell_draw(splits[2], (SECTIONS, D, EXPERTS), D ** -0.5, 0.109375, ((0, 2),), jnp.float32)
    w_gate = bell_draw(splits[3], (SECTIONS, SLICES * EXPERTS, D, FF_DEV), D ** -0.5, 0.109375, ((0, 2), (1, 8)))
    w_up = bell_draw(splits[4], (SECTIONS, SLICES * EXPERTS, D, FF_DEV), D ** -0.5, 0.109375, ((0, 2), (1, 8)))
    w_down = bell_draw(splits[5], (SECTIONS, SLICES * EXPERTS, FF_DEV, D), FF ** -0.5, 0.0625, ((0, 2), (1, 8)))
    routes_keys = jax.random.split(jax.random.fold_in(own_keys[6], 1), SECTIONS * TOKENS // ROWS_DEV)
    routes_turns = jax.random.permutation(jax.random.fold_in(own_keys[6], 3), SECTIONS * TOKENS // ROWS_DEV)
    routes = jax.vmap(lambda own, number: routed_block(jax.random.fold_in(own_keys[6], 2), own, number, ROWS_DEV, EXPERTS, 2, ROWS_DEV, 2))(routes_keys, routes_turns).reshape((SECTIONS, TOKENS, 2))
    return {"token_rows": token_rows, "norm_gain": norm_gain, "router": router, "w_gate": w_gate, "w_up": w_up, "w_down": w_down, "routes": routes}


epsilon = 1e-05

def normalize(residual, gain):
    values = residual.astype(jnp.float32)
    inv_rms = lax.rsqrt(lax.optimization_barrier(jnp.mean(values * values, axis=-1, keepdims=True)) + epsilon)
    return (values * inv_rms * gain).astype(jnp.bfloat16)

def mixing_weights(normed, router_cols, pair):
    logits = jnp.dot(normed.astype(jnp.float32), router_cols, precision=lax.Precision.HIGHEST)
    expert_ids = jnp.arange(router_cols.shape[1], dtype=jnp.int32)
    first_hit = (pair[:, 0:1] == expert_ids[None, :]).astype(jnp.float32)
    second_hit = (pair[:, 1:2] == expert_ids[None, :]).astype(jnp.float32)
    first_logit = lax.optimization_barrier(jnp.sum(logits * first_hit, axis=1))
    second_logit = lax.optimization_barrier(jnp.sum(logits * second_hit, axis=1))
    first_gate = 1.0 / (1.0 + jnp.exp(second_logit - first_logit))
    second_gate = 1.0 / (1.0 + jnp.exp(first_logit - second_logit))
    member = first_hit + second_hit
    mixing = first_hit * first_gate[:, None] + second_hit * second_gate[:, None]
    return (member, mixing)

def moe_layer(residual, gain, router_cols, pair, gate_all, up_all, down_all):
    normed = normalize(residual, gain)
    mixing = mixing_weights(normed, router_cols, pair)[1]
    branch = jnp.zeros(residual.shape, jnp.float32)
    for expert in range(EXPERTS):
        gate_full = jnp.transpose(gate_all.reshape(SLICES, EXPERTS, D, FF_DEV)[:, expert], (1, 0, 2)).reshape(D, FF)
        up_full = jnp.transpose(up_all.reshape(SLICES, EXPERTS, D, FF_DEV)[:, expert], (1, 0, 2)).reshape(D, FF)
        down_full = down_all.reshape(SLICES, EXPERTS, FF_DEV, D)[:, expert].reshape(FF, D)
        gate_proj = jnp.dot(normed, gate_full, preferred_element_type=jnp.float32)
        up_proj = jnp.dot(normed, up_full, preferred_element_type=jnp.float32)
        hidden = (jax.nn.silu(gate_proj) * up_proj).astype(jnp.bfloat16)
        expert_out = jnp.dot(hidden, down_full, preferred_element_type=jnp.float32)
        branch = branch + mixing[:, expert:expert + 1] * expert_out
    return (residual.astype(jnp.float32) + branch).astype(jnp.bfloat16)

def reference(token_rows, norm_gain, router, w_gate, w_up, w_down, routes):
    results = [moe_layer(token_rows[section_id], norm_gain[section_id], router[section_id], routes[section_id], w_gate[section_id], w_up[section_id], w_down[section_id]) for section_id in range(SECTIONS)]
    return jnp.roll(jnp.stack(results), 1, axis=0)
```

```python
import functools

import jax
import jax.numpy as jnp
from jax import lax
from jax.experimental import pallas as pl
from jax.experimental.pallas import tpu as pltpu
from jax.sharding import PartitionSpec as P

epsilon = 1e-05
MESH = pl.DeviceIdType.MESH


def each(count, start, body):
    if count <= 8:
        for i in range(start, count):
            body(i)
    else:
        def step(i, carry):
            body(i)
            return carry

        lax.fori_loop(start, count, step, 0)


def kernel(
    cfg,
    x_hbm, gain_hbm, router_hbm, routes_ref, gate_hbm, up_hbm, down_hbm,
    out_ref,
    x_ref, gain_ref, router_ref, first_col, second_col,
    gathered, pool, gate_acc, up_acc, hidden, weights, mixing,
    send_y, own, recv_y, send_z, recv_z, resid,
    small_sem, pool_sem, res_sem, az_send, az_recv, ay_send, ay_recv,
    ry_send, ry_recv, rz_send, rz_recv, mz_send, mz_recv, my_sem, ao_sem,
):
    nz, rows, kc, nk, ff, ft, nc, cw, lag, ahead, experts, units, early = cfg
    tokens = 2 * nz * rows
    half = nz * rows
    tiles = ff // ft
    subs = ft // cw
    per_chunk = ff // (kc * subs)
    gate_units = nk * tiles * 2
    all_units = gate_units + nc * per_chunk
    position = lax.axis_index("expert")
    section = lax.axis_index("section")
    z, y = position // 2, position % 2
    expert = position % experts
    other = 1 - section

    def ring(value):
        return lax.rem(value + nz, nz)

    def rows_at(start):
        if isinstance(start, int):
            return pl.ds(start * rows, rows)
        return pl.ds(pl.multiple_of(start * rows, rows), rows)

    def start_unit(g):
        slot = g % units
        if g < gate_units:
            k, t, src = g // (2 * tiles), g // 2 % tiles, (gate_hbm, up_hbm)[g % 2]
            pltpu.make_async_copy(
                src.at[0, 0, pl.ds(k * kc, kc), pl.ds(t * ft, ft)], pool.at[slot], pool_sem.at[slot]).start()
            return
        c, part = (g - gate_units) // per_chunk, (g - gate_units) % per_chunk
        for b in range(subs):
            pltpu.make_async_copy(
                down_hbm.at[0, 0, pl.ds((part * subs + b) * kc, kc), pl.ds(c * cw, cw)],
                pool.at[slot, :, pl.ds(b * cw, cw)], pool_sem.at[slot]).start()

    def wait_unit(slot):
        pltpu.make_async_copy(
            gate_hbm.at[0, 0, pl.ds(0, kc), pl.ds(0, ft)], pool.at[slot], pool_sem.at[slot]).wait()

    def along_z(k, j):
        return pltpu.make_async_remote_copy(
            src_ref=gathered.at[k, rows_at(0), :], dst_ref=gathered.at[k, rows_at(j), :],
            send_sem=az_send.at[k, j], recv_sem=az_recv.at[k, j],
            device_id={"expert": ring(z + j) * 2 + y}, device_id_type=MESH)

    def own_along_y():
        return pltpu.make_async_remote_copy(
            src_ref=gathered.at[:, rows_at(0), :], dst_ref=gathered.at[:, rows_at(nz), :],
            send_sem=ao_sem.at[0], recv_sem=ao_sem.at[1],
            device_id={"expert": z * 2 + 1 - y}, device_id_type=MESH)

    def along_y(k):
        return pltpu.make_async_remote_copy(
            src_ref=gathered.at[k, pl.ds(rows, half - rows), :],
            dst_ref=gathered.at[k, pl.ds(half + rows, half - rows), :],
            send_sem=ay_send.at[k], recv_sem=ay_recv.at[k],
            device_id={"expert": z * 2 + 1 - y}, device_id_type=MESH)

    def weights_z(j):
        return pltpu.make_async_remote_copy(
            src_ref=weights.at[rows_at(0), :], dst_ref=weights.at[rows_at(j), :],
            send_sem=mz_send.at[j], recv_sem=mz_recv.at[j],
            device_id={"expert": ring(z + j) * 2 + y}, device_id_type=MESH)

    def weights_y():
        return pltpu.make_async_remote_copy(
            src_ref=weights.at[0:half, :], dst_ref=weights.at[half:2 * half, :],
            send_sem=my_sem.at[0], recv_sem=my_sem.at[1],
            device_id={"expert": z * 2 + 1 - y}, device_id_type=MESH)

    def reduce_y(c):
        return pltpu.make_async_remote_copy(
            src_ref=send_y.at[c], dst_ref=recv_y.at[c],
            send_sem=ry_send.at[c], recv_sem=ry_recv.at[c],
            device_id={"expert": z * 2 + 1 - y}, device_id_type=MESH)

    def reduce_z(c, j):
        return pltpu.make_async_remote_copy(
            src_ref=send_z.at[c, rows_at((nz - j) % nz), :], dst_ref=recv_z.at[c, j],
            send_sem=rz_send.at[c, j], recv_sem=rz_recv.at[c, j],
            device_id={"section": other, "expert": ring(z + j) * 2 + y}, device_id_type=MESH)

    small = [
        pltpu.make_async_copy(src, dst, small_sem.at[i])
        for i, (src, dst) in enumerate(
            ((x_hbm, x_ref), (gain_hbm, gain_ref), (router_hbm, router_ref)))
    ]
    for copy in small:
        copy.start()

    barrier = pltpu.get_barrier_semaphore()

    def greet_z(j):
        pl.semaphore_signal(
            barrier, inc=1, device_id={"expert": ring(z + j) * 2 + y}, device_id_type=MESH)

    def greet_other(j):
        pl.semaphore_signal(
            barrier, inc=1, device_id={"section": other, "expert": ring(z + j) * 2 + y},
            device_id_type=MESH)

    each(nz, 1, greet_z)
    each(nz, 0, greet_other)
    pl.semaphore_signal(
        barrier, inc=1, device_id={"expert": z * 2 + 1 - y}, device_id_type=MESH)
    for g in range(early):
        start_unit(g)

    small[0].wait()
    small[1].wait()
    values = x_ref[0].astype(jnp.float32)
    inv_rms = lax.rsqrt(jnp.mean(values * values, axis=-1, keepdims=True) + epsilon)
    for k in range(nk):
        cols = slice(k * kc, (k + 1) * kc)
        gathered[k, rows_at(0), :] = (values[:, cols] * inv_rms * gain_ref[:, cols]).astype(jnp.bfloat16)

    pl.semaphore_wait(barrier, 2 * nz)
    for k in range(nk):
        each(nz, 1, lambda j: along_z(k, j).start())
        if k == 0:
            own_along_y().start()
    res_copy = pltpu.make_async_remote_copy(
        src_ref=x_ref, dst_ref=resid, send_sem=res_sem.at[0], recv_sem=res_sem.at[1],
        device_id={"section": other}, device_id_type=MESH)
    res_copy.start()
    for g in range(early, units):
        start_unit(g)

    def forward(k):
        each(nz, 1, lambda j: along_z(k, j).wait_recv())
        along_y(k).start()

    small[2].wait()
    ids = routes_ref[...].astype(jnp.float32)
    first_col[...] = jnp.transpose(jnp.broadcast_to(ids[0:1], (8, tokens)))
    second_col[...] = jnp.transpose(jnp.broadcast_to(ids[1:2], (8, tokens)))
    first = first_col[rows_at(position), 0:1]
    second = second_col[rows_at(position), 0:1]
    own_logits = [jnp.zeros((rows, 1), jnp.float32) for _ in range(experts)]
    for k in range(nk):
        normed = gathered[k, rows_at(0), :].astype(jnp.float32)
        for e in range(experts):
            own_logits[e] = own_logits[e] + jnp.sum(
                normed * router_ref[e:e + 1, k * kc:(k + 1) * kc], axis=1, keepdims=True)
    first_logit = jnp.zeros((rows, 1), jnp.float32)
    second_logit = jnp.zeros((rows, 1), jnp.float32)
    for e in range(experts):
        first_logit = jnp.where(first == e, own_logits[e], first_logit)
        second_logit = jnp.where(second == e, own_logits[e], second_logit)
    first_gate = 1.0 / (1.0 + jnp.exp(second_logit - first_logit))
    second_gate = 1.0 / (1.0 + jnp.exp(first_logit - second_logit))
    lane = lax.broadcasted_iota(jnp.int32, (rows, 128), 1).astype(jnp.float32)
    weights[rows_at(0), :] = jnp.where(lane == first, first_gate, 0.0) + jnp.where(
        lane == second, second_gate, 0.0)
    each(nz, 1, lambda j: weights_z(j).start())

    for k in range(min(ahead, nk)):
        forward(k)
    for k in range(nk):
        if k + ahead < nk:
            forward(k + ahead)
        if k == nk - 1:
            each(nz, 1, lambda j: weights_z(j).wait_recv())
            weights_y().start()
        if k == 0:
            own_along_y().wait_recv()
        along_y(k).wait_recv()

        def tile(t, carry):
            cols = pl.ds(pl.multiple_of(t * ft, ft), ft)
            slot = (k * tiles * 2) % units + 2 * t
            wait_unit(slot)
            wait_unit(slot + 1)
            lhs = gathered[k]
            gate = jnp.dot(lhs, pool[slot], preferred_element_type=jnp.float32)
            up = jnp.dot(lhs, pool[slot + 1], preferred_element_type=jnp.float32)
            if k > 0:
                gate = gate + gate_acc[:, cols]
                up = up + up_acc[:, cols]
            if k < nk - 1:
                gate_acc[:, cols] = gate
                up_acc[:, cols] = up
            else:
                hidden[:, cols] = (gate / (1.0 + jnp.exp(-gate)) * up).astype(jnp.bfloat16)
            return carry

        lax.fori_loop(0, tiles, tile, 0)
        for g in range(units + k * tiles * 2, min(units + (k + 1) * tiles * 2, all_units)):
            start_unit(g)

    weights_y().wait_recv()
    lane = lax.broadcasted_iota(jnp.int32, (tokens, 128), 1)
    weight = jnp.sum(jnp.where(lane == expert, weights[...], 0.0), axis=1, keepdims=True)
    mixing[...] = jnp.broadcast_to(weight, (tokens, 128))

    def second_stage(c):
        reduce_y(c).wait_recv()
        send_z[c] = (own[c] + recv_y[c].astype(jnp.float32)).astype(jnp.bfloat16)
        each(nz, 0, lambda j: reduce_z(c, j).start())

    def down(c, carry):
        blocks = []
        for part in range(per_chunk):
            slot = lax.rem(gate_units + c * per_chunk + part, units)
            wait_unit(slot)
            blocks += [pool[slot, :, b * cw:(b + 1) * cw] for b in range(subs)]
        part = jnp.dot(hidden[...], jnp.concatenate(blocks, axis=0), preferred_element_type=jnp.float32)
        part = part * mixing[:, 0:1]
        send_y[c] = part[half:].astype(jnp.bfloat16)
        reduce_y(c).start()
        own[c] = part[:half]

        @pl.when(c >= lag)
        def _():
            second_stage(c - lag)

        return carry

    lax.fori_loop(0, nc, down, 0)
    for c in range(nc - lag, nc):
        second_stage(c)
    res_copy.wait_recv()
    for c in range(nc):
        cols = slice(c * cw, (c + 1) * cw)
        each(nz, 0, lambda j: reduce_z(c, j).wait_recv())
        branch = jnp.sum(recv_z[c].astype(jnp.float32), axis=0)
        out_ref[0, :, cols] = (resid[0, :, cols].astype(jnp.float32) + branch).astype(jnp.bfloat16)

    res_copy.wait_send()
    own_along_y().wait_send()
    each(nz, 1, lambda j: weights_z(j).wait_send())
    weights_y().wait_send()
    for k in range(nk):
        each(nz, 1, lambda j: along_z(k, j).wait_send())
        along_y(k).wait_send()

    def drain(c, carry):
        reduce_y(c).wait_send()
        each(nz, 0, lambda j: reduce_z(c, j).wait_send())
        return carry

    lax.fori_loop(0, nc, drain, 0)


def body(token_rows, norm_gain, router, w_gate, w_up, w_down, routes):
    _, rows, features = token_rows.shape
    ff = w_gate.shape[3]
    experts = router.shape[2]
    nz = lax.axis_size("expert") // 2
    total = 2 * nz * rows
    half = nz * rows
    kc, cw = 512, 512
    nk, nc = features // kc, features // cw
    lag, ahead = 3, 2
    ft = min(2048, ff)
    total_units = nk * (ff // ft) * 2 + nc * (ff // (kc * (ft // cw)))
    units, early = min(24, total_units), 6
    cfg = (nz, rows, kc, nk, ff, ft, nc, cw, lag, ahead, experts, units, early)
    vmem = pl.BlockSpec(memory_space=pltpu.VMEM)
    hbm = pl.BlockSpec(memory_space=pl.ANY)
    bf16, f32 = jnp.bfloat16, jnp.float32
    dma = pltpu.SemaphoreType.DMA
    return pl.pallas_call(
        functools.partial(kernel, cfg),
        out_shape=jax.ShapeDtypeStruct((1, rows, features), bf16),
        in_specs=[hbm] * 3 + [vmem] + [hbm] * 3,
        out_specs=vmem,
        scratch_shapes=[
            pltpu.VMEM((1, rows, features), bf16),
            pltpu.VMEM((1, features), f32),
            pltpu.VMEM((experts, features), f32),
            pltpu.VMEM((total, 8), f32),
            pltpu.VMEM((total, 8), f32),
            pltpu.VMEM((nk, total, kc), bf16),
            pltpu.VMEM((units, kc, ft), bf16),
            pltpu.VMEM((total, ff), f32),
            pltpu.VMEM((total, ff), f32),
            pltpu.VMEM((total, ff), bf16),
            pltpu.VMEM((total, 128), f32),
            pltpu.VMEM((total, 128), f32),
            pltpu.VMEM((nc, half, cw), bf16),
            pltpu.VMEM((nc, half, cw), f32),
            pltpu.VMEM((nc, half, cw), bf16),
            pltpu.VMEM((nc, half, cw), bf16),
            pltpu.VMEM((nc, nz, rows, cw), bf16),
            pltpu.VMEM((1, rows, features), bf16),
            dma((3,)), dma((units,)), dma((2,)),
            dma((nk, nz)), dma((nk, nz)), dma((nk,)), dma((nk,)),
            dma((nc,)), dma((nc,)), dma((nc, nz)), dma((nc, nz)),
            dma((nz,)), dma((nz,)), dma((2,)), dma((2,)),
        ],
        compiler_params=pltpu.CompilerParams(
            collective_id=0, has_side_effects=True, vmem_limit_bytes=62 * 2**20),
    )(token_rows, norm_gain, router[0].T, routes[0].T, w_gate, w_up, w_down)


def solution(mesh):
    in_specs = (
        P("section", ("groups", "expert"), None),
        P("section", None),
        P("section", None, None),
        P("section", "expert", None, None),
        P("section", "expert", None, None),
        P("section", "expert", None, None),
        P("section", "groups", None),
    )
    out_specs = P("section", ("groups", "expert"), None)
    return jax.shard_map(body, mesh=mesh, in_specs=in_specs, out_specs=out_specs, check_vma=False)
```

```python
import functools
import math

import jax
import jax.numpy as jnp
from jax import lax
from jax.experimental import pallas as pl
from jax.experimental.pallas import tpu as pltpu
from jax.sharding import PartitionSpec as P

epsilon = 1e-05
MESH = pl.DeviceIdType.MESH


def each(count, start, body):
    if count <= 8:
        for i in range(start, count):
            body(i)
    else:
        def step(i, carry):
            body(i)
            return carry

        lax.fori_loop(start, count, step, 0)


def kernel(
    cfg,
    x_hbm, gain_hbm, router_hbm, routes_hbm, gate_hbm, up_hbm, down_hbm,
    out_ref,
    x_ref, gain_ref, router_ref, routes_ref, first_col, second_col,
    gathered, pool, gate_acc, up_acc, hidden, weights, mixing,
    send_y, own, recv_y, send_z, recv_z, resid,
    small_sem, pool_sem, res_sem, az_send, az_recv, ay_send, ay_recv,
    ry_send, ry_recv, rz_send, rz_recv, mz_send, mz_recv, my_sem, ao_sem,
):
    nz, rows, kc, nk, ff, ft, nc, cw, bw, pieces, late, outs, lag, ahead, experts, units, early = cfg
    tokens = 2 * nz * rows
    half = nz * rows
    tiles = ff // ft
    subs = ft // cw
    per_chunk = ff // (kc * subs)
    gate_units = nk * tiles * 2
    all_units = gate_units + nc * per_chunk
    blocks = nk * kc // bw
    ready = len(pieces) - late
    position = lax.axis_index("expert")
    section = lax.axis_index("section")
    z, y = position // 2, position % 2
    expert = position % experts
    other = 1 - section

    def ring(value):
        return lax.rem(value + nz, nz)

    def rows_at(start):
        if isinstance(start, int):
            return pl.ds(start * rows, rows)
        return pl.ds(pl.multiple_of(start * rows, rows), rows)

    def start_unit(g):
        slot = g % units
        if g < gate_units:
            k, t, src = g // (2 * tiles), g // 2 % tiles, (gate_hbm, up_hbm)[g % 2]
            pltpu.make_async_copy(
                src.at[0, 0, pl.ds(k * kc, kc), pl.ds(t * ft, ft)], pool.at[slot], pool_sem.at[slot]).start()
            return
        c, part = (g - gate_units) // per_chunk, (g - gate_units) % per_chunk
        for b in range(subs):
            pltpu.make_async_copy(
                down_hbm.at[0, 0, pl.ds((part * subs + b) * kc, kc), pl.ds(c * cw, cw)],
                pool.at[slot, :, pl.ds(b * cw, cw)], pool_sem.at[slot]).start()

    def wait_unit(slot):
        pltpu.make_async_copy(
            gate_hbm.at[0, 0, pl.ds(0, kc), pl.ds(0, ft)], pool.at[slot], pool_sem.at[slot]).wait()

    def cut(i):
        return pl.ds(pieces[i][0], pieces[i][1])

    def along_z(i, j):
        side = pl.ds(0, 1 if i < ready else 2)
        return pltpu.make_async_remote_copy(
            src_ref=gathered.at[cut(i), side, rows_at(0), :], dst_ref=gathered.at[cut(i), side, rows_at(j), :],
            send_sem=az_send.at[i, j], recv_sem=az_recv.at[i, j],
            device_id={"expert": ring(z + j) * 2 + y}, device_id_type=MESH)

    def own_along_y(part):
        first = pieces[ready][0] if late else blocks
        span = (pl.ds(0, first), pl.ds(first, blocks - first))[part]
        return pltpu.make_async_remote_copy(
            src_ref=gathered.at[span, 0, rows_at(0), :], dst_ref=gathered.at[span, 1, rows_at(0), :],
            send_sem=ao_sem.at[0, part], recv_sem=ao_sem.at[1, part],
            device_id={"expert": z * 2 + 1 - y}, device_id_type=MESH)

    def along_y(i):
        return pltpu.make_async_remote_copy(
            src_ref=gathered.at[cut(i), 0, pl.ds(rows, half - rows), :],
            dst_ref=gathered.at[cut(i), 1, pl.ds(rows, half - rows), :],
            send_sem=ay_send.at[i], recv_sem=ay_recv.at[i],
            device_id={"expert": z * 2 + 1 - y}, device_id_type=MESH)

    def weights_z(j):
        return pltpu.make_async_remote_copy(
            src_ref=weights.at[rows_at(0), :], dst_ref=weights.at[rows_at(j), :],
            send_sem=mz_send.at[j], recv_sem=mz_recv.at[j],
            device_id={"expert": ring(z + j) * 2 + y}, device_id_type=MESH)

    def weights_y():
        return pltpu.make_async_remote_copy(
            src_ref=weights.at[0:half, :], dst_ref=weights.at[half:2 * half, :],
            send_sem=my_sem.at[0], recv_sem=my_sem.at[1],
            device_id={"expert": z * 2 + 1 - y}, device_id_type=MESH)

    def span(p):
        return pl.ds(outs[p][0], outs[p][1])

    def reduce_y(p):
        return pltpu.make_async_remote_copy(
            src_ref=send_y.at[span(p)], dst_ref=recv_y.at[span(p)],
            send_sem=ry_send.at[p], recv_sem=ry_recv.at[p],
            device_id={"expert": z * 2 + 1 - y}, device_id_type=MESH)

    def reduce_z(p, j):
        return pltpu.make_async_remote_copy(
            src_ref=send_z.at[span(p), rows_at((nz - j) % nz), :], dst_ref=recv_z.at[j, span(p)],
            send_sem=rz_send.at[p, j], recv_sem=rz_recv.at[p, j],
            device_id={"section": other, "expert": ring(z + j) * 2 + y}, device_id_type=MESH)

    small = [
        pltpu.make_async_copy(src, dst, small_sem.at[i])
        for i, (src, dst) in enumerate(
            ((x_hbm, x_ref), (gain_hbm, gain_ref), (router_hbm, router_ref), (routes_hbm, routes_ref)))
    ]
    for copy in small:
        copy.start()

    barrier = pltpu.get_barrier_semaphore()

    def greet_z(j):
        pl.semaphore_signal(
            barrier, inc=1, device_id={"expert": ring(z + j) * 2 + y}, device_id_type=MESH)

    def greet_other(j):
        pl.semaphore_signal(
            barrier, inc=1, device_id={"section": other, "expert": ring(z + j) * 2 + y},
            device_id_type=MESH)

    each(nz, 1, greet_z)
    each(nz, 0, greet_other)
    pl.semaphore_signal(
        barrier, inc=1, device_id={"expert": z * 2 + 1 - y}, device_id_type=MESH)
    for g in range(early):
        start_unit(g)

    small[0].wait()
    small[1].wait()
    values = x_ref[0].astype(jnp.float32)
    inv_rms = lax.rsqrt(jnp.mean(values * values, axis=-1, keepdims=True) + epsilon)
    for b in range(blocks):
        cols = slice(b * bw, (b + 1) * bw)
        gathered[b, 0, rows_at(0), :] = (values[:, cols] * inv_rms * gain_ref[:, cols]).astype(jnp.bfloat16)

    pl.semaphore_wait(barrier, 2 * nz)
    for i in range(ready):
        each(nz, 1, lambda j: along_z(i, j).start())
        if i == 0:
            if late:
                own_along_y(1).start()
            own_along_y(0).start()
    res_copy = pltpu.make_async_remote_copy(
        src_ref=x_ref, dst_ref=resid, send_sem=res_sem.at[0], recv_sem=res_sem.at[1],
        device_id={"section": other}, device_id_type=MESH)
    res_copy.start()
    for g in range(early, units):
        start_unit(g)

    def forward(i):
        if i < ready:
            each(nz, 1, lambda j: along_z(i, j).wait_recv())
            along_y(i).start()

    small[2].wait()
    small[3].wait()
    ids = routes_ref[...].astype(jnp.float32)
    first_col[...] = jnp.transpose(jnp.broadcast_to(ids[0:1], (8, tokens)))
    second_col[...] = jnp.transpose(jnp.broadcast_to(ids[1:2], (8, tokens)))
    first = first_col[rows_at(position), 0:1]
    second = second_col[rows_at(position), 0:1]
    own_logits = [jnp.zeros((rows, 1), jnp.float32) for _ in range(experts)]
    for b in range(blocks):
        normed = gathered[b, 0, rows_at(0), :].astype(jnp.float32)
        for e in range(experts):
            own_logits[e] = own_logits[e] + jnp.sum(
                normed * router_ref[e:e + 1, b * bw:(b + 1) * bw], axis=1, keepdims=True)
    first_logit = jnp.zeros((rows, 1), jnp.float32)
    second_logit = jnp.zeros((rows, 1), jnp.float32)
    for e in range(experts):
        first_logit = jnp.where(first == e, own_logits[e], first_logit)
        second_logit = jnp.where(second == e, own_logits[e], second_logit)
    first_gate = 1.0 / (1.0 + jnp.exp(second_logit - first_logit))
    second_gate = 1.0 / (1.0 + jnp.exp(first_logit - second_logit))
    lane = lax.broadcasted_iota(jnp.int32, (rows, 128), 1).astype(jnp.float32)
    weights[rows_at(0), :] = jnp.where(lane == first, first_gate, 0.0) + jnp.where(
        lane == second, second_gate, 0.0)
    each(nz, 1, lambda j: weights_z(j).start())

    if late:
        own_along_y(1).wait_recv()
        for i in range(ready, len(pieces)):
            each(nz, 1, lambda j: along_z(i, j).start())
    sent = arrived = 0
    for k in range(nk):
        last = [i for i, (block, count) in enumerate(pieces) if block * bw < (k + 1) * kc][-1] + 1
        while sent < min(last + ahead, len(pieces)):
            forward(sent)
            sent += 1
        if k == nk - 1:
            each(nz, 1, lambda j: weights_z(j).wait_recv())
            weights_y().start()
        if k == 0:
            own_along_y(0).wait_recv()
        for i in range(arrived, last):
            if i < ready:
                along_y(i).wait_recv()
            else:
                each(nz, 1, lambda j: along_z(i, j).wait_recv())
        arrived = last

        def tile(t, carry):
            cols = pl.ds(pl.multiple_of(t * ft, ft), ft)
            slot = (k * tiles * 2) % units + 2 * t
            wait_unit(slot)
            wait_unit(slot + 1)
            lhs = jnp.concatenate(
                [gathered[b].reshape(tokens, bw) for b in range(k * kc // bw, (k + 1) * kc // bw)], axis=1)
            gate = jnp.dot(lhs, pool[slot], preferred_element_type=jnp.float32)
            up = jnp.dot(lhs, pool[slot + 1], preferred_element_type=jnp.float32)
            if k > 0:
                gate = gate + gate_acc[:, cols]
                up = up + up_acc[:, cols]
            if k < nk - 1:
                gate_acc[:, cols] = gate
                up_acc[:, cols] = up
            else:
                hidden[:, cols] = (gate / (1.0 + jnp.exp(-gate)) * up).astype(jnp.bfloat16)
            return carry

        lax.fori_loop(0, tiles, tile, 0)
        for g in range(units + k * tiles * 2, min(units + (k + 1) * tiles * 2, all_units)):
            start_unit(g)

    weights_y().wait_recv()
    lane = lax.broadcasted_iota(jnp.int32, (tokens, 128), 1)
    weight = jnp.sum(jnp.where(lane == expert, weights[...], 0.0), axis=1, keepdims=True)
    mixing[...] = jnp.broadcast_to(weight, (tokens, 128))

    def second_stage(p):
        reduce_y(p).wait_recv()
        for b in range(outs[p][0], outs[p][0] + outs[p][1]):
            send_z[b] = (own[b] + recv_y[b].astype(jnp.float32)).astype(jnp.bfloat16)
        each(nz, 0, lambda j: reduce_z(p, j).start())

    def down(c):
        parts = []
        for part in range(per_chunk):
            slot = (gate_units + c * per_chunk + part) % units
            if not isinstance(c, int):
                slot = lax.rem(gate_units + c * per_chunk + part, units)
            wait_unit(slot)
            parts += [pool[slot, :, b * cw:(b + 1) * cw] for b in range(subs)]
        product = jnp.dot(hidden[...], jnp.concatenate(parts, axis=0), preferred_element_type=jnp.float32)
        product = product * mixing[:, 0:1]
        for b in range(cw // bw):
            send_y[c * (cw // bw) + b] = product[half:, b * bw:(b + 1) * bw].astype(jnp.bfloat16)
            own[c * (cw // bw) + b] = product[:half, b * bw:(b + 1) * bw]

    p = 0
    for c in range(nc):
        down(c)
        while p < len(outs) and (outs[p][0] + outs[p][1]) * bw <= (c + 1) * cw:
            reduce_y(p).start()
            if p >= lag:
                second_stage(p - lag)
            p += 1
    for p in range(len(outs) - lag, len(outs)):
        second_stage(p)
    res_copy.wait_recv()
    for p, (block, count) in enumerate(outs):
        each(nz, 0, lambda j: reduce_z(p, j).wait_recv())
        for b in range(block, block + count):
            cols = slice(b * bw, (b + 1) * bw)
            branch = jnp.sum(recv_z[:, b].astype(jnp.float32), axis=0)
            out_ref[0, :, cols] = (resid[0, :, cols].astype(jnp.float32) + branch).astype(jnp.bfloat16)

    res_copy.wait_send()
    for part in range(2 if late else 1):
        own_along_y(part).wait_send()
    each(nz, 1, lambda j: weights_z(j).wait_send())
    weights_y().wait_send()
    for i in range(len(pieces)):
        each(nz, 1, lambda j: along_z(i, j).wait_send())
        if i < ready:
            along_y(i).wait_send()
    for p in range(len(outs)):
        reduce_y(p).wait_send()
        each(nz, 0, lambda j: reduce_z(p, j).wait_send())


def body(token_rows, norm_gain, router, w_gate, w_up, w_down, routes):
    _, rows, features = token_rows.shape
    ff = w_gate.shape[3]
    experts = router.shape[2]
    nz = lax.axis_size("expert") // 2
    total = 2 * nz * rows
    half = nz * rows
    kc, cw = 512, 512
    nk, nc = features // kc, features // cw
    bw, lag, ahead, late = 256, 4, 2, 1
    blocks = features // bw
    pieces = [(b, 2) for b in range(0, blocks, 2)]
    outs = [(b, 2) for b in range(0, blocks, 2)]
    np, no = len(pieces), len(outs)
    ft = min(2048, ff)
    total_units = nk * (ff // ft) * 2 + nc * (ff // (kc * (ft // cw)))
    units, early = min(20, total_units), 6
    cfg = (nz, rows, kc, nk, ff, ft, nc, cw, bw, pieces, late, outs, lag, ahead, experts, units, early)
    vmem = pl.BlockSpec(memory_space=pltpu.VMEM)
    hbm = pl.BlockSpec(memory_space=pltpu.HBM)
    bf16, f32 = jnp.bfloat16, jnp.float32
    dma = pltpu.SemaphoreType.DMA
    held = [
        ((1, rows, features), bf16),
        ((1, features), f32),
        ((experts, features), f32),
        ((2, total), jnp.int32),
        ((total, 8), f32),
        ((total, 8), f32),
        ((blocks, 2, half, bw), bf16),
        ((units, kc, ft), bf16),
        ((total, ff), f32),
        ((total, ff), f32),
        ((total, ff), bf16),
        ((total, 128), f32),
        ((total, 128), f32),
        ((blocks, half, bw), bf16),
        ((blocks, half, bw), f32),
        ((blocks, half, bw), bf16),
        ((blocks, half, bw), bf16),
        ((nz, blocks, rows, bw), bf16),
        ((1, rows, features), bf16),
    ]
    limit = (52 if total <= 256 else 62) * 2**20
    return pl.pallas_call(
        functools.partial(kernel, cfg),
        out_shape=jax.ShapeDtypeStruct((1, rows, features), bf16),
        in_specs=[hbm] * 7,
        out_specs=vmem,
        scratch_shapes=[pltpu.VMEM(*shape) for shape in held] + [
            dma((4,)), dma((units,)), dma((2,)),
            dma((np, nz)), dma((np, nz)), dma((np,)), dma((np,)),
            dma((no,)), dma((no,)), dma((no, nz)), dma((no, nz)),
            dma((nz,)), dma((nz,)), dma((2,)), dma((2, 2)),
        ],
        compiler_params=pltpu.CompilerParams(
            collective_id=0, has_side_effects=True, vmem_limit_bytes=limit),
    )(*[pltpu.with_memory_space_constraint(a, pltpu.HBM) for a in (token_rows, norm_gain, router[0].T, routes[0].T)], w_gate, w_up, w_down)


def solution(mesh):
    in_specs = (
        P("section", ("groups", "expert"), None),
        P("section", None),
        P("section", None, None),
        P("section", "expert", None, None),
        P("section", "expert", None, None),
        P("section", "expert", None, None),
        P("section", "groups", None),
    )
    out_specs = P("section", ("groups", "expert"), None)
    return jax.shard_map(body, mesh=mesh, in_specs=in_specs, out_specs=out_specs, check_vma=False)
```

```python
import functools
import math

import jax
import jax.numpy as jnp
from jax import lax
from jax.experimental import pallas as pl
from jax.experimental.pallas import tpu as pltpu
from jax.sharding import PartitionSpec as P

epsilon = 1e-05
MESH = pl.DeviceIdType.MESH


def each(count, start, body):
    if count <= 8:
        for i in range(start, count):
            body(i)
    else:
        def step(i, carry):
            body(i)
            return carry

        lax.fori_loop(start, count, step, 0)


def kernel(
    cfg,
    x_hbm, gain_hbm, router_hbm, routes_hbm, gate_hbm, up_hbm, down_hbm,
    out_ref,
    x_ref, gain_ref, router_ref, routes_ref, first_col, second_col,
    gathered, pool, gate_acc, up_acc, hidden, weights, mixing,
    send_y, own, recv_y, send_z, recv_z, resid,
    small_sem, pool_sem, res_sem, az_send, az_recv, ay_send, ay_recv,
    ry_send, ry_recv, rz_send, rz_recv, mz_send, mz_recv, my_sem, ao_sem,
):
    nz, rows, kc, nk, ff, ft, nc, cw, bw, pieces, late, outs, lag, ahead, experts, units, early = cfg
    tokens = 2 * nz * rows
    half = nz * rows
    tiles = ff // ft
    subs = ft // cw
    per_chunk = ff // (kc * subs)
    gate_units = nk * tiles * 2
    all_units = gate_units + nc * per_chunk
    blocks = nk * kc // bw
    ready = len(pieces) - late
    position = lax.axis_index("expert")
    section = lax.axis_index("section")
    z, y = position // 2, position % 2
    expert = position % experts
    other = 1 - section

    def ring(value):
        return lax.rem(value + nz, nz)

    def rows_at(start):
        if isinstance(start, int):
            return pl.ds(start * rows, rows)
        return pl.ds(pl.multiple_of(start * rows, rows), rows)

    def start_unit(g):
        slot = g % units
        if g < gate_units:
            k, t, src = g // (2 * tiles), g // 2 % tiles, (gate_hbm, up_hbm)[g % 2]
            pltpu.make_async_copy(
                src.at[0, 0, pl.ds(k * kc, kc), pl.ds(t * ft, ft)], pool.at[slot], pool_sem.at[slot]).start()
            return
        c, part = (g - gate_units) // per_chunk, (g - gate_units) % per_chunk
        for b in range(subs):
            pltpu.make_async_copy(
                down_hbm.at[0, 0, pl.ds((part * subs + b) * kc, kc), pl.ds(c * cw, cw)],
                pool.at[slot, :, pl.ds(b * cw, cw)], pool_sem.at[slot]).start()

    def wait_unit(slot):
        pltpu.make_async_copy(
            gate_hbm.at[0, 0, pl.ds(0, kc), pl.ds(0, ft)], pool.at[slot], pool_sem.at[slot]).wait()

    def cut(i):
        return pl.ds(pieces[i][0], pieces[i][1])

    def along_z(i, j):
        side = pl.ds(0, 1 if i < ready else 2)
        return pltpu.make_async_remote_copy(
            src_ref=gathered.at[cut(i), side, rows_at(0), :], dst_ref=gathered.at[cut(i), side, rows_at(j), :],
            send_sem=az_send.at[i, j], recv_sem=az_recv.at[i, j],
            device_id={"expert": ring(z + j) * 2 + y}, device_id_type=MESH)

    def own_along_y(part):
        first = pieces[ready][0] if late else blocks
        span = (pl.ds(0, first), pl.ds(first, blocks - first))[part]
        return pltpu.make_async_remote_copy(
            src_ref=gathered.at[span, 0, rows_at(0), :], dst_ref=gathered.at[span, 1, rows_at(0), :],
            send_sem=ao_sem.at[0, part], recv_sem=ao_sem.at[1, part],
            device_id={"expert": z * 2 + 1 - y}, device_id_type=MESH)

    def along_y(i):
        return pltpu.make_async_remote_copy(
            src_ref=gathered.at[cut(i), 0, pl.ds(rows, half - rows), :],
            dst_ref=gathered.at[cut(i), 1, pl.ds(rows, half - rows), :],
            send_sem=ay_send.at[i], recv_sem=ay_recv.at[i],
            device_id={"expert": z * 2 + 1 - y}, device_id_type=MESH)

    def weights_z(j):
        return pltpu.make_async_remote_copy(
            src_ref=weights.at[rows_at(0), :], dst_ref=weights.at[rows_at(j), :],
            send_sem=mz_send.at[j], recv_sem=mz_recv.at[j],
            device_id={"expert": ring(z + j) * 2 + y}, device_id_type=MESH)

    def weights_y():
        return pltpu.make_async_remote_copy(
            src_ref=weights.at[0:half, :], dst_ref=weights.at[half:2 * half, :],
            send_sem=my_sem.at[0], recv_sem=my_sem.at[1],
            device_id={"expert": z * 2 + 1 - y}, device_id_type=MESH)

    def span(p):
        return pl.ds(outs[p][0], outs[p][1])

    def reduce_y(p):
        return pltpu.make_async_remote_copy(
            src_ref=send_y.at[span(p)], dst_ref=recv_y.at[span(p)],
            send_sem=ry_send.at[p], recv_sem=ry_recv.at[p],
            device_id={"expert": z * 2 + 1 - y}, device_id_type=MESH)

    def reduce_z(p, j):
        return pltpu.make_async_remote_copy(
            src_ref=send_z.at[span(p), rows_at((nz - j) % nz), :], dst_ref=recv_z.at[j, span(p)],
            send_sem=rz_send.at[p, j], recv_sem=rz_recv.at[p, j],
            device_id={"section": other, "expert": ring(z + j) * 2 + y}, device_id_type=MESH)

    small = [
        pltpu.make_async_copy(src, dst, small_sem.at[i])
        for i, (src, dst) in enumerate(
            ((x_hbm, x_ref), (gain_hbm, gain_ref), (router_hbm, router_ref), (routes_hbm, routes_ref)))
    ]
    for copy in small:
        copy.start()

    barrier = pltpu.get_barrier_semaphore()

    def greet_z(j):
        pl.semaphore_signal(
            barrier, inc=1, device_id={"expert": ring(z + j) * 2 + y}, device_id_type=MESH)

    def greet_other(j):
        pl.semaphore_signal(
            barrier, inc=1, device_id={"section": other, "expert": ring(z + j) * 2 + y},
            device_id_type=MESH)

    each(nz, 1, greet_z)
    each(nz, 0, greet_other)
    pl.semaphore_signal(
        barrier, inc=1, device_id={"expert": z * 2 + 1 - y}, device_id_type=MESH)
    for g in range(early):
        start_unit(g)

    small[0].wait()
    small[1].wait()
    values = x_ref[0].astype(jnp.float32)
    inv_rms = lax.rsqrt(jnp.mean(values * values, axis=-1, keepdims=True) + epsilon)
    for b in range(blocks):
        cols = slice(b * bw, (b + 1) * bw)
        gathered[b, 0, rows_at(0), :] = (values[:, cols] * inv_rms * gain_ref[:, cols]).astype(jnp.bfloat16)

    pl.semaphore_wait(barrier, 2 * nz)
    for i in range(ready):
        each(nz, 1, lambda j: along_z(i, j).start())
        if i == 0:
            if late:
                own_along_y(1).start()
            own_along_y(0).start()
    res_copy = pltpu.make_async_remote_copy(
        src_ref=x_ref, dst_ref=resid, send_sem=res_sem.at[0], recv_sem=res_sem.at[1],
        device_id={"section": other}, device_id_type=MESH)
    res_copy.start()
    for g in range(early, units):
        start_unit(g)

    def forward(i):
        if i < ready:
            each(nz, 1, lambda j: along_z(i, j).wait_recv())
            along_y(i).start()

    small[2].wait()
    small[3].wait()
    ids = routes_ref[...].astype(jnp.float32)
    first_col[...] = jnp.transpose(jnp.broadcast_to(ids[0:1], (8, tokens)))
    second_col[...] = jnp.transpose(jnp.broadcast_to(ids[1:2], (8, tokens)))
    first = first_col[rows_at(position), 0:1]
    second = second_col[rows_at(position), 0:1]
    own_logits = [jnp.zeros((rows, 1), jnp.float32) for _ in range(experts)]
    for b in range(blocks):
        normed = gathered[b, 0, rows_at(0), :].astype(jnp.float32)
        for e in range(experts):
            own_logits[e] = own_logits[e] + jnp.sum(
                normed * router_ref[e:e + 1, b * bw:(b + 1) * bw], axis=1, keepdims=True)
    first_logit = jnp.zeros((rows, 1), jnp.float32)
    second_logit = jnp.zeros((rows, 1), jnp.float32)
    for e in range(experts):
        first_logit = jnp.where(first == e, own_logits[e], first_logit)
        second_logit = jnp.where(second == e, own_logits[e], second_logit)
    first_gate = 1.0 / (1.0 + jnp.exp(second_logit - first_logit))
    second_gate = 1.0 / (1.0 + jnp.exp(first_logit - second_logit))
    lane = lax.broadcasted_iota(jnp.int32, (rows, 128), 1).astype(jnp.float32)
    weights[rows_at(0), :] = jnp.where(lane == first, first_gate, 0.0) + jnp.where(
        lane == second, second_gate, 0.0)
    each(nz, 1, lambda j: weights_z(j).start())

    if late:
        own_along_y(1).wait_recv()
        for i in range(ready, len(pieces)):
            each(nz, 1, lambda j: along_z(i, j).start())
    sent = arrived = 0
    for k in range(nk):
        last = [i for i, (block, count) in enumerate(pieces) if block * bw < (k + 1) * kc][-1] + 1
        while sent < min(last + ahead, len(pieces)):
            forward(sent)
            sent += 1
        if k == nk - 1:
            each(nz, 1, lambda j: weights_z(j).wait_recv())
            weights_y().start()
        if k == 0:
            own_along_y(0).wait_recv()
        for i in range(arrived, last):
            if i < ready:
                along_y(i).wait_recv()
            else:
                each(nz, 1, lambda j: along_z(i, j).wait_recv())
        arrived = last

        base = (k * tiles * 2) % units
        for slot in range(base, base + 2 * tiles):
            wait_unit(slot)
        lhs = jnp.concatenate(
            [gathered[b].reshape(tokens, bw) for b in range(k * kc // bw, (k + 1) * kc // bw)], axis=1)
        gate, up = (
            jnp.dot(
                lhs, jnp.concatenate([pool[base + 2 * t + side] for t in range(tiles)], axis=1),
                preferred_element_type=jnp.float32)
            for side in (0, 1))
        if k > 0:
            gate = gate + gate_acc[...]
            up = up + up_acc[...]
        if k < nk - 1:
            gate_acc[...] = gate
            up_acc[...] = up
        else:
            hidden[...] = (gate / (1.0 + jnp.exp(-gate)) * up).astype(jnp.bfloat16)
        for g in range(units + k * tiles * 2, min(units + (k + 1) * tiles * 2, all_units)):
            start_unit(g)

    weights_y().wait_recv()
    lane = lax.broadcasted_iota(jnp.int32, (tokens, 128), 1)
    weight = jnp.sum(jnp.where(lane == expert, weights[...], 0.0), axis=1, keepdims=True)
    mixing[...] = jnp.broadcast_to(weight, (tokens, 128))

    def second_stage(p):
        reduce_y(p).wait_recv()
        for b in range(outs[p][0], outs[p][0] + outs[p][1]):
            send_z[b] = (own[b] + recv_y[b].astype(jnp.float32)).astype(jnp.bfloat16)
        each(nz, 1, lambda j: reduce_z(p, j).start())
        reduce_z(p, 0).start()

    def down(c):
        parts = []
        for part in range(per_chunk):
            slot = (gate_units + c * per_chunk + part) % units
            if not isinstance(c, int):
                slot = lax.rem(gate_units + c * per_chunk + part, units)
            wait_unit(slot)
            parts += [pool[slot, :, b * cw:(b + 1) * cw] for b in range(subs)]
        product = jnp.dot(hidden[...], jnp.concatenate(parts, axis=0), preferred_element_type=jnp.float32)
        product = product * mixing[:, 0:1]
        for b in range(cw // bw):
            send_y[c * (cw // bw) + b] = product[half:, b * bw:(b + 1) * bw].astype(jnp.bfloat16)
            own[c * (cw // bw) + b] = product[:half, b * bw:(b + 1) * bw]

    p = 0
    for c in range(nc):
        down(c)
        while p < len(outs) and (outs[p][0] + outs[p][1]) * bw <= (c + 1) * cw:
            reduce_y(p).start()
            if p >= lag:
                second_stage(p - lag)
            p += 1
    for p in range(len(outs) - lag, len(outs)):
        second_stage(p)
    res_copy.wait_recv()
    for p, (block, count) in enumerate(outs):
        each(nz, 0, lambda j: reduce_z(p, j).wait_recv())
        for b in range(block, block + count):
            cols = slice(b * bw, (b + 1) * bw)
            branch = jnp.sum(recv_z[:, b].astype(jnp.float32), axis=0)
            out_ref[0, :, cols] = (resid[0, :, cols].astype(jnp.float32) + branch).astype(jnp.bfloat16)

    res_copy.wait_send()
    for part in range(2 if late else 1):
        own_along_y(part).wait_send()
    each(nz, 1, lambda j: weights_z(j).wait_send())
    weights_y().wait_send()
    for i in range(len(pieces)):
        each(nz, 1, lambda j: along_z(i, j).wait_send())
        if i < ready:
            along_y(i).wait_send()
    for p in range(len(outs)):
        reduce_y(p).wait_send()
        each(nz, 0, lambda j: reduce_z(p, j).wait_send())


def body(token_rows, norm_gain, router, w_gate, w_up, w_down, routes):
    _, rows, features = token_rows.shape
    ff = w_gate.shape[3]
    experts = router.shape[2]
    nz = lax.axis_size("expert") // 2
    total = 2 * nz * rows
    half = nz * rows
    kc, cw = 512, 512
    nk, nc = features // kc, features // cw
    bw, lag, ahead, late = 256, 4, 2, 2
    blocks = features // bw
    pieces = [(b, 2) for b in range(0, blocks, 2)]
    outs = [(b, 2) for b in range(0, blocks, 2)]
    np, no = len(pieces), len(outs)
    ft = min(2048, ff)
    total_units = nk * (ff // ft) * 2 + nc * (ff // (kc * (ft // cw)))
    units, early = min(16, total_units), 6
    cfg = (nz, rows, kc, nk, ff, ft, nc, cw, bw, pieces, late, outs, lag, ahead, experts, units, early)
    vmem = pl.BlockSpec(memory_space=pltpu.VMEM)
    hbm = pl.BlockSpec(memory_space=pltpu.HBM)
    bf16, f32 = jnp.bfloat16, jnp.float32
    dma = pltpu.SemaphoreType.DMA
    held = [
        ((1, rows, features), bf16),
        ((1, features), f32),
        ((experts, features), f32),
        ((2, total), jnp.int32),
        ((total, 8), f32),
        ((total, 8), f32),
        ((blocks, 2, half, bw), bf16),
        ((units, kc, ft), bf16),
        ((total, ff), f32),
        ((total, ff), f32),
        ((total, ff), bf16),
        ((total, 128), f32),
        ((total, 128), f32),
        ((blocks, half, bw), bf16),
        ((blocks, half, bw), f32),
        ((blocks, half, bw), bf16),
        ((blocks, half, bw), bf16),
        ((nz, blocks, rows, bw), bf16),
        ((1, rows, features), bf16),
    ]
    limit = (52 if total <= 256 else 62) * 2**20
    return pl.pallas_call(
        functools.partial(kernel, cfg),
        out_shape=jax.ShapeDtypeStruct((1, rows, features), bf16),
        in_specs=[hbm] * 7,
        out_specs=vmem,
        scratch_shapes=[pltpu.VMEM(*shape) for shape in held] + [
            dma((4,)), dma((units,)), dma((2,)),
            dma((np, nz)), dma((np, nz)), dma((np,)), dma((np,)),
            dma((no,)), dma((no,)), dma((no, nz)), dma((no, nz)),
            dma((nz,)), dma((nz,)), dma((2,)), dma((2, 2)),
        ],
        compiler_params=pltpu.CompilerParams(
            collective_id=0, has_side_effects=True, vmem_limit_bytes=limit),
    )(*[pltpu.with_memory_space_constraint(a, pltpu.HBM) for a in (token_rows, norm_gain, router[0].T, routes[0].T)], w_gate, w_up, w_down)


def solution(mesh):
    in_specs = (
        P("section", ("groups", "expert"), None),
        P("section", None),
        P("section", None, None),
        P("section", "expert", None, None),
        P("section", "expert", None, None),
        P("section", "expert", None, None),
        P("section", "groups", None),
    )
    out_specs = P("section", ("groups", "expert"), None)
    return jax.shard_map(body, mesh=mesh, in_specs=in_specs, out_specs=out_specs, check_vma=False)
```

```python
import functools
import math

import jax
import jax.numpy as jnp
from jax import lax
from jax.experimental import pallas as pl
from jax.experimental.pallas import tpu as pltpu
from jax.sharding import PartitionSpec as P

epsilon = 1e-05
MESH = pl.DeviceIdType.MESH


def each(count, start, body):
    if count <= 8:
        for i in range(start, count):
            body(i)
    else:
        def step(i, carry):
            body(i)
            return carry

        lax.fori_loop(start, count, step, 0)


def kernel(
    cfg,
    x_hbm, gain_hbm, router_hbm, routes_hbm, gate_hbm, up_hbm, down_hbm,
    out_ref,
    x_ref, gain_ref, router_ref, routes_ref, first_col, second_col,
    gathered, pool, gate_acc, up_acc, hidden, weights, mixing,
    send_y, own, recv_y, send_z, recv_z, resid,
    small_sem, pool_sem, res_sem, az_send, az_recv, ay_send, ay_recv,
    ry_send, ry_recv, rz_send, rz_recv, mz_send, mz_recv, my_sem, ao_sem,
):
    nz, rows, kc, nk, ff, ft, nc, cw, bw, pieces, late, outs, lag, ahead, experts, units, early = cfg
    tokens = 2 * nz * rows
    half = nz * rows
    tiles = ff // ft
    subs = ft // cw
    per_chunk = ff // (kc * subs)
    gate_units = nk * tiles * 2
    all_units = gate_units + nc * per_chunk
    blocks = nk * kc // bw
    ready = len(pieces) - late
    position = lax.axis_index("expert")
    section = lax.axis_index("section")
    z, y = position // 2, position % 2
    expert = position % experts
    other = 1 - section

    def ring(value):
        return lax.rem(value + nz, nz)

    def rows_at(start):
        if isinstance(start, int):
            return pl.ds(start * rows, rows)
        return pl.ds(pl.multiple_of(start * rows, rows), rows)

    def start_unit(g):
        slot = g % units
        if g < gate_units:
            k, t, src = g // (2 * tiles), g // 2 % tiles, (gate_hbm, up_hbm)[g % 2]
            pltpu.make_async_copy(
                src.at[0, 0, pl.ds(k * kc, kc), pl.ds(t * ft, ft)], pool.at[slot], pool_sem.at[slot]).start()
            return
        c, part = (g - gate_units) // per_chunk, (g - gate_units) % per_chunk
        for b in range(subs):
            pltpu.make_async_copy(
                down_hbm.at[0, 0, pl.ds((part * subs + b) * kc, kc), pl.ds(c * cw, cw)],
                pool.at[slot, :, pl.ds(b * cw, cw)], pool_sem.at[slot]).start()

    def wait_unit(slot):
        pltpu.make_async_copy(
            gate_hbm.at[0, 0, pl.ds(0, kc), pl.ds(0, ft)], pool.at[slot], pool_sem.at[slot]).wait()

    def cut(i):
        return pl.ds(pieces[i][0], pieces[i][1])

    def along_z(i, j):
        side = pl.ds(0, 1 if i < ready else 2)
        return pltpu.make_async_remote_copy(
            src_ref=gathered.at[cut(i), side, rows_at(0), :], dst_ref=gathered.at[cut(i), side, rows_at(j), :],
            send_sem=az_send.at[i, j], recv_sem=az_recv.at[i, j],
            device_id={"expert": ring(z + j) * 2 + y}, device_id_type=MESH)

    def own_along_y(part):
        first = pieces[ready][0] if late else blocks
        span = (pl.ds(0, first), pl.ds(first, blocks - first))[part]
        return pltpu.make_async_remote_copy(
            src_ref=gathered.at[span, 0, rows_at(0), :], dst_ref=gathered.at[span, 1, rows_at(0), :],
            send_sem=ao_sem.at[0, part], recv_sem=ao_sem.at[1, part],
            device_id={"expert": z * 2 + 1 - y}, device_id_type=MESH)

    def along_y(i):
        return pltpu.make_async_remote_copy(
            src_ref=gathered.at[cut(i), 0, pl.ds(rows, half - rows), :],
            dst_ref=gathered.at[cut(i), 1, pl.ds(rows, half - rows), :],
            send_sem=ay_send.at[i], recv_sem=ay_recv.at[i],
            device_id={"expert": z * 2 + 1 - y}, device_id_type=MESH)

    def weights_z(j):
        return pltpu.make_async_remote_copy(
            src_ref=weights.at[rows_at(0), :], dst_ref=weights.at[rows_at(j), :],
            send_sem=mz_send.at[j], recv_sem=mz_recv.at[j],
            device_id={"expert": ring(z + j) * 2 + y}, device_id_type=MESH)

    def weights_y():
        return pltpu.make_async_remote_copy(
            src_ref=weights.at[0:half, :], dst_ref=weights.at[half:2 * half, :],
            send_sem=my_sem.at[0], recv_sem=my_sem.at[1],
            device_id={"expert": z * 2 + 1 - y}, device_id_type=MESH)

    def span(p):
        return pl.ds(outs[p][0], outs[p][1])

    def reduce_y(p):
        return pltpu.make_async_remote_copy(
            src_ref=send_y.at[span(p)], dst_ref=recv_y.at[span(p)],
            send_sem=ry_send.at[p], recv_sem=ry_recv.at[p],
            device_id={"expert": z * 2 + 1 - y}, device_id_type=MESH)

    def reduce_z(p, j):
        return pltpu.make_async_remote_copy(
            src_ref=send_z.at[span(p), rows_at((nz - j) % nz), :], dst_ref=recv_z.at[j, span(p)],
            send_sem=rz_send.at[p, j], recv_sem=rz_recv.at[p, j],
            device_id={"section": other, "expert": ring(z + j) * 2 + y}, device_id_type=MESH)

    small = [
        pltpu.make_async_copy(src, dst, small_sem.at[i])
        for i, (src, dst) in enumerate(
            ((x_hbm, x_ref), (gain_hbm, gain_ref), (router_hbm, router_ref), (routes_hbm, routes_ref)))
    ]
    for copy in small:
        copy.start()

    barrier = pltpu.get_barrier_semaphore()

    def greet_z(j):
        pl.semaphore_signal(
            barrier, inc=1, device_id={"expert": ring(z + j) * 2 + y}, device_id_type=MESH)

    def greet_other(j):
        pl.semaphore_signal(
            barrier, inc=1, device_id={"section": other, "expert": ring(z + j) * 2 + y},
            device_id_type=MESH)

    each(nz, 1, greet_z)
    each(nz, 0, greet_other)
    pl.semaphore_signal(
        barrier, inc=1, device_id={"expert": z * 2 + 1 - y}, device_id_type=MESH)
    for g in range(early):
        start_unit(g)

    small[0].wait()
    small[1].wait()
    values = x_ref[0].astype(jnp.float32)
    inv_rms = lax.rsqrt(jnp.mean(values * values, axis=-1, keepdims=True) + epsilon)
    for b in range(blocks):
        cols = slice(b * bw, (b + 1) * bw)
        gathered[b, 0, rows_at(0), :] = (values[:, cols] * inv_rms * gain_ref[:, cols]).astype(jnp.bfloat16)

    pl.semaphore_wait(barrier, 2 * nz)
    for i in range(ready):
        each(nz, 1, lambda j: along_z(i, j).start())
        if i == 0:
            if late:
                own_along_y(1).start()
            own_along_y(0).start()
    res_copy = pltpu.make_async_remote_copy(
        src_ref=x_ref, dst_ref=resid, send_sem=res_sem.at[0], recv_sem=res_sem.at[1],
        device_id={"section": other}, device_id_type=MESH)
    res_copy.start()
    for g in range(early, units):
        start_unit(g)

    def forward(i):
        if i < ready:
            each(nz, 1, lambda j: along_z(i, j).wait_recv())
            along_y(i).start()

    small[2].wait()
    small[3].wait()
    ids = routes_ref[...].astype(jnp.float32)
    first_col[...] = jnp.transpose(jnp.broadcast_to(ids[0:1], (8, tokens)))
    second_col[...] = jnp.transpose(jnp.broadcast_to(ids[1:2], (8, tokens)))
    first = first_col[rows_at(position), 0:1]
    second = second_col[rows_at(position), 0:1]
    own_logits = [jnp.zeros((rows, 1), jnp.float32) for _ in range(experts)]
    for b in range(blocks):
        normed = gathered[b, 0, rows_at(0), :].astype(jnp.float32)
        for e in range(experts):
            own_logits[e] = own_logits[e] + jnp.sum(
                normed * router_ref[e:e + 1, b * bw:(b + 1) * bw], axis=1, keepdims=True)
    first_logit = jnp.zeros((rows, 1), jnp.float32)
    second_logit = jnp.zeros((rows, 1), jnp.float32)
    for e in range(experts):
        first_logit = jnp.where(first == e, own_logits[e], first_logit)
        second_logit = jnp.where(second == e, own_logits[e], second_logit)
    first_gate = 1.0 / (1.0 + jnp.exp(second_logit - first_logit))
    second_gate = 1.0 / (1.0 + jnp.exp(first_logit - second_logit))
    lane = lax.broadcasted_iota(jnp.int32, (rows, 128), 1).astype(jnp.float32)
    weights[rows_at(0), :] = jnp.where(lane == first, first_gate, 0.0) + jnp.where(
        lane == second, second_gate, 0.0)
    each(nz, 1, lambda j: weights_z(j).start())

    if late:
        own_along_y(1).wait_recv()
        for i in range(ready, len(pieces)):
            each(nz, 1, lambda j: along_z(i, j).start())
    sent = arrived = 0
    for k in range(nk):
        last = [i for i, (block, count) in enumerate(pieces) if block * bw < (k + 1) * kc][-1] + 1
        while sent < min(last + ahead, len(pieces)):
            forward(sent)
            sent += 1
        if k == nk - 1:
            each(nz, 1, lambda j: weights_z(j).wait_recv())
            weights_y().start()
        if k == 0:
            own_along_y(0).wait_recv()
        for i in range(arrived, last):
            if i < ready:
                along_y(i).wait_recv()
            else:
                each(nz, 1, lambda j: along_z(i, j).wait_recv())
        arrived = last

        base = (k * tiles * 2) % units
        for slot in range(base, base + 2 * tiles):
            wait_unit(slot)
        lhs = jnp.concatenate(
            [gathered[b].reshape(tokens, bw) for b in range(k * kc // bw, (k + 1) * kc // bw)], axis=1)
        gate, up = (
            jnp.dot(
                lhs, jnp.concatenate([pool[base + 2 * t + side] for t in range(tiles)], axis=1),
                preferred_element_type=jnp.float32)
            for side in (0, 1))
        if k > 0:
            gate = gate + gate_acc[...]
            up = up + up_acc[...]
        if k < nk - 1:
            gate_acc[...] = gate
            up_acc[...] = up
        else:
            hidden[...] = (gate / (1.0 + jnp.exp(-gate)) * up).astype(jnp.bfloat16)
        for g in range(units + k * tiles * 2, min(units + (k + 1) * tiles * 2, all_units)):
            start_unit(g)

    weights_y().wait_recv()
    lane = lax.broadcasted_iota(jnp.int32, (tokens, 128), 1)
    weight = jnp.sum(jnp.where(lane == expert, weights[...], 0.0), axis=1, keepdims=True)
    mixing[...] = jnp.broadcast_to(weight, (tokens, 128))

    def second_stage(p):
        reduce_y(p).wait_recv()
        for b in range(outs[p][0], outs[p][0] + outs[p][1]):
            send_z[b] = (own[b] + recv_y[b].astype(jnp.float32)).astype(jnp.bfloat16)
        each(nz, 1, lambda j: reduce_z(p, j).start())
        reduce_z(p, 0).start()

    def down(c):
        parts = []
        for part in range(per_chunk):
            slot = (gate_units + c * per_chunk + part) % units
            if not isinstance(c, int):
                slot = lax.rem(gate_units + c * per_chunk + part, units)
            wait_unit(slot)
            parts += [pool[slot, :, b * cw:(b + 1) * cw] for b in range(subs)]
        matrix = jnp.concatenate(parts, axis=0)
        if c == 0:
            away = jnp.dot(hidden[half:, :], matrix, preferred_element_type=jnp.float32) * mixing[half:, 0:1]
            for b in range(cw // bw):
                send_y[b] = away[:, b * bw:(b + 1) * bw].astype(jnp.bfloat16)
            reduce_y(0).start()
            kept = jnp.dot(hidden[:half, :], matrix, preferred_element_type=jnp.float32) * mixing[:half, 0:1]
            for b in range(cw // bw):
                own[b] = kept[:, b * bw:(b + 1) * bw]
            return
        product = jnp.dot(hidden[...], matrix, preferred_element_type=jnp.float32)
        product = product * mixing[:, 0:1]
        for b in range(cw // bw):
            send_y[c * (cw // bw) + b] = product[half:, b * bw:(b + 1) * bw].astype(jnp.bfloat16)
            own[c * (cw // bw) + b] = product[:half, b * bw:(b + 1) * bw]

    p = 0
    for c in range(nc):
        down(c)
        while p < len(outs) and (outs[p][0] + outs[p][1]) * bw <= (c + 1) * cw:
            if p > 0:
                reduce_y(p).start()
            if p >= lag:
                second_stage(p - lag)
            p += 1
    for p in range(len(outs) - lag, len(outs)):
        second_stage(p)
    res_copy.wait_recv()
    for p, (block, count) in enumerate(outs):
        each(nz, 0, lambda j: reduce_z(p, j).wait_recv())
        for b in range(block, block + count):
            cols = slice(b * bw, (b + 1) * bw)
            branch = jnp.sum(recv_z[:, b].astype(jnp.float32), axis=0)
            out_ref[0, :, cols] = (resid[0, :, cols].astype(jnp.float32) + branch).astype(jnp.bfloat16)

    res_copy.wait_send()
    for part in range(2 if late else 1):
        own_along_y(part).wait_send()
    each(nz, 1, lambda j: weights_z(j).wait_send())
    weights_y().wait_send()
    for i in range(len(pieces)):
        each(nz, 1, lambda j: along_z(i, j).wait_send())
        if i < ready:
            along_y(i).wait_send()
    for p in range(len(outs)):
        reduce_y(p).wait_send()
        each(nz, 0, lambda j: reduce_z(p, j).wait_send())


def body(token_rows, norm_gain, router, w_gate, w_up, w_down, routes):
    _, rows, features = token_rows.shape
    ff = w_gate.shape[3]
    experts = router.shape[2]
    nz = lax.axis_size("expert") // 2
    total = 2 * nz * rows
    half = nz * rows
    kc, cw = 512, 512
    nk, nc = features // kc, features // cw
    bw, lag, ahead, late = 256, 4, 2, 2
    blocks = features // bw
    pieces = [(b, 2) for b in range(0, blocks, 2)]
    outs = [(b, 2) for b in range(0, blocks, 2)]
    np, no = len(pieces), len(outs)
    ft = min(2048, ff)
    total_units = nk * (ff // ft) * 2 + nc * (ff // (kc * (ft // cw)))
    units, early = min(16, total_units), 6
    cfg = (nz, rows, kc, nk, ff, ft, nc, cw, bw, pieces, late, outs, lag, ahead, experts, units, early)
    vmem = pl.BlockSpec(memory_space=pltpu.VMEM)
    hbm = pl.BlockSpec(memory_space=pltpu.HBM)
    bf16, f32 = jnp.bfloat16, jnp.float32
    dma = pltpu.SemaphoreType.DMA
    held = [
        ((1, rows, features), bf16),
        ((1, features), f32),
        ((experts, features), f32),
        ((2, total), jnp.int32),
        ((total, 8), f32),
        ((total, 8), f32),
        ((blocks, 2, half, bw), bf16),
        ((units, kc, ft), bf16),
        ((total, ff), f32),
        ((total, ff), f32),
        ((total, ff), bf16),
        ((total, 128), f32),
        ((total, 128), f32),
        ((blocks, half, bw), bf16),
        ((blocks, half, bw), f32),
        ((blocks, half, bw), bf16),
        ((blocks, half, bw), bf16),
        ((nz, blocks, rows, bw), bf16),
        ((1, rows, features), bf16),
    ]
    limit = (52 if total <= 256 else 62) * 2**20
    return pl.pallas_call(
        functools.partial(kernel, cfg),
        out_shape=jax.ShapeDtypeStruct((1, rows, features), bf16),
        in_specs=[hbm] * 7,
        out_specs=vmem,
        scratch_shapes=[pltpu.VMEM(*shape) for shape in held] + [
            dma((4,)), dma((units,)), dma((2,)),
            dma((np, nz)), dma((np, nz)), dma((np,)), dma((np,)),
            dma((no,)), dma((no,)), dma((no, nz)), dma((no, nz)),
            dma((nz,)), dma((nz,)), dma((2,)), dma((2, 2)),
        ],
        compiler_params=pltpu.CompilerParams(
            collective_id=0, has_side_effects=True, vmem_limit_bytes=limit),
    )(*[pltpu.with_memory_space_constraint(a, pltpu.HBM) for a in (token_rows, norm_gain, router[0].T, routes[0].T)], w_gate, w_up, w_down)


def solution(mesh):
    in_specs = (
        P("section", ("groups", "expert"), None),
        P("section", None),
        P("section", None, None),
        P("section", "expert", None, None),
        P("section", "expert", None, None),
        P("section", "expert", None, None),
        P("section", "groups", None),
    )
    out_specs = P("section", ("groups", "expert"), None)
    return jax.shard_map(body, mesh=mesh, in_specs=in_specs, out_specs=out_specs, check_vma=False)
```
